32 devices in a mesh: dp: 4 (over z), vocab: 8 (over y, x, core).
Axes of the slice: x: 2, y: 2, z: 4, core: 2. Of those that a mesh axis runs over, the one named last changes fastest.
Arguments:
- teacher_logits: bfloat16 [512, 64000], P('dp', 'vocab'), may hold values from -64 to 320
- student_hidden: bfloat16 [512, 2304], P('dp'), may hold values from -100 to 100
- student_head: bfloat16 [2304, 16384], P('dp', 'vocab'), may hold values from -0.625 to 0.625
- keep_ids: int32 [128, 128], replicated, may hold values from -1 to 63999, as said below
- block_owner: int32 [128], replicated, may hold values from 0 to 7, as said below
- block_count: int32 [128], replicated, may hold values from 32 to 128
Outputs:
- head_grad: bfloat16 [2304, 16384], P('dp', 'vocab')
- hidden_grad: bfloat16 [512, 2304], P(('dp', 'vocab'))
The draws below stay inside these ranges and needn't reach their ends.
Inputs may be any that keep to these rules, and one draw needn't show every extreme that they name: `keep_ids`: lanes below block_count[b] hold ids, the others -1. The ids of the whole table increase along each block and from block to block, and the ids of one block lie in one range of 8000 ids (the same id // 8000). One such range holds at most 32 blocks. `block_owner`: every vocab index owns exactly 16 blocks. The blocks of one range of 8000 ids owned by one vocab index number at most 4, and some pair reaches 4.
All inputs are finite; a program needn't handle non-finite values.
Results may differ from the reference program's by a relative error of at most 0.0049.
Values may be sent and summed in bfloat16 or wider, within the bound.
No kernel may reach another device: no remote copies, remote signals or barrier semaphores. Data moves between devices by JAX's collectives and lax.ppermute only.
A program may use at most 64 MiB of HBM per device.

```python
import math
import jax
import jax.numpy as jnp
from jax import lax

D = 2304
VT_DEV = 8000
KB_DEV = 16
BLOCK = 128
TOKENS = 512
VOCAB = 64000
NB = 128
KEPT = 16384
N_VOCAB = 8


def block_tables(key):
    subkeys = jax.random.split(jax.random.fold_in(key, 7), 8)
    shard_count = N_VOCAB
    pairing = jax.random.permutation(subkeys[0], shard_count)
    shifted = jax.random.randint(subkeys[1], (shard_count // 2,), 0, KB_DEV + 1)
    shifted = shifted.at[0].set(KB_DEV)
    change = jnp.zeros((shard_count,), jnp.int32).at[pairing[0::2]].set(shifted).at[pairing[1::2]].set(-shifted)
    per_shard = KB_DEV + change
    shard_ends = jnp.cumsum(per_shard)
    numbers = jnp.arange(NB, dtype=jnp.int32)
    source = jnp.sum((shard_ends[None, :] <= numbers[:, None]).astype(jnp.int32), axis=1)
    counts = jax.random.randint(subkeys[2], (NB,), BLOCK // 4, BLOCK + 1)
    full_block = jax.random.randint(subkeys[3], (), 0, NB)
    short_block = (full_block + 1 + jax.random.randint(subkeys[7], (), 0, NB - 1)) % NB
    counts = counts.at[full_block].set(BLOCK).at[short_block].set(BLOCK // 4)
    earlier_same = (source[None, :] == source[:, None]) & (numbers[None, :] < numbers[:, None])
    offset = jnp.sum(jnp.where(earlier_same, counts[None, :], 0), axis=1)
    totals = jax.ops.segment_sum(counts, source, shard_count)
    id_ranks = jax.vmap(lambda single: jax.random.permutation(single, VT_DEV))(jax.random.split(subkeys[4], shard_count))
    chosen = id_ranks < totals[:, None]
    sorted_ids = jnp.argsort(jnp.where(chosen, 0, 1), axis=1, stable=True).astype(jnp.int32)
    lane_index = jnp.arange(BLOCK, dtype=jnp.int32)
    position = jnp.minimum(offset[:, None] + lane_index[None, :], VT_DEV - 1)
    local_ids = sorted_ids[source[:, None], position]
    kept_ids = jnp.where(lane_index[None, :] < counts[:, None], source[:, None] * VT_DEV + local_ids, -1)
    owner_order = jax.random.permutation(subkeys[5], shard_count)
    rotation = jax.random.randint(subkeys[6], (), 0, shard_count)
    owners = owner_order[(numbers + rotation) % shard_count]
    return (kept_ids.astype(jnp.int32), owners.astype(jnp.int32), counts.astype(jnp.int32))


def draw_keep_ids(key, part):
    return block_tables(key)[0]


def draw_block_owner(key, part):
    return block_tables(key)[1]


def draw_block_count(key, part):
    return block_tables(key)[2]


def student_pair(key):
    subkeys = jax.random.split(jax.random.fold_in(key, 11), 9)
    column_scale = jnp.exp(jax.random.uniform(subkeys[0], (KEPT,), minval=math.log(0.5), maxval=math.log(1.5)))
    row_scale = jnp.exp(jax.random.uniform(subkeys[1], (TOKENS,), minval=math.log(0.1), maxval=0.0))
    owner_rise = (jnp.arange(KEPT, dtype=jnp.int32) // (KB_DEV * BLOCK)).astype(jnp.float32) / (N_VOCAB - 1)
    bias_row = 0.5 * owner_rise * jax.random.uniform(subkeys[7], (KEPT,), minval=0.8, maxval=1.2)
    base_noise = jnp.clip(jax.random.normal(subkeys[5], (TOKENS, D)), -6.0, 6.0)
    lead = jax.random.uniform(subkeys[8], (TOKENS,), minval=2.0, maxval=2.6)
    head_matrix = jnp.clip(jax.random.normal(subkeys[6], (D, KEPT)), -6.0, 6.0) * column_scale[None, :] / math.sqrt(D)
    head_matrix = head_matrix.at[0].set(bias_row)
    hidden = base_noise * row_scale[:, None]
    hidden = hidden.at[:, 0].set(lead)
    return (hidden, head_matrix)


def draw_student_hidden(key, part):
    return student_pair(key)[0].astype(jnp.bfloat16)


def draw_student_head(key, part):
    return student_pair(key)[1].astype(jnp.bfloat16)


def draw_teacher_logits(key, part):
    subkeys = jax.random.split(jax.random.fold_in(key, 23), 3)
    row_scale = jnp.exp(jax.random.uniform(subkeys[0], (TOKENS,), minval=math.log(0.1), maxval=0.0))
    column_scale = jnp.exp(jax.random.uniform(subkeys[1], (VOCAB,), minval=0.0, maxval=math.log(1.5)))
    kept_ids, owners, counts = block_tables(key)
    vocab_index = jnp.arange(VOCAB, dtype=jnp.int32)
    shard_rise = (vocab_index // VT_DEV).astype(jnp.float32) / (N_VOCAB - 1)
    targets = jnp.where(kept_ids >= 0, kept_ids, VOCAB).reshape(-1)
    owner_rise = jnp.broadcast_to(owners[:, None].astype(jnp.float32) / (N_VOCAB - 1), (NB, BLOCK)).reshape(-1)
    kept_rise = jnp.zeros((VOCAB,), jnp.float32).at[targets].set(owner_rise, mode='drop')
    base_noise = jnp.clip(jax.random.normal(subkeys[2], (TOKENS, VOCAB)), -5.0, 5.0)
    lift = math.log(3.0)
    logits = base_noise * row_scale[:, None] * column_scale[None, :] + lift * (shard_rise + kept_rise)[None, :]
    return logits.astype(jnp.bfloat16)


def setup_inputs(seed: int = 0) -> dict:
    streams_of = jax.random.split(jax.random.key(seed), 7)
    return {
        "teacher_logits": draw_teacher_logits(jax.random.fold_in(streams_of[6], 71), 0),
        "student_hidden": draw_student_hidden(jax.random.fold_in(streams_of[6], 71), 0),
        "student_head": draw_student_head(jax.random.fold_in(streams_of[6], 71), 0),
        "keep_ids": draw_keep_ids(jax.random.fold_in(streams_of[6], 71), 0),
        "block_owner": draw_block_owner(jax.random.fold_in(streams_of[6], 71), 0),
        "block_count": draw_block_count(jax.random.fold_in(streams_of[6], 71), 0),
    }


loss_scale = 8192.0


def student_layout(block_owner):
    numbers = jnp.arange(NB, dtype=jnp.int32)
    earlier = (block_owner[None, :] == block_owner[:, None]) & (numbers[None, :] < numbers[:, None])
    ordinal = jnp.sum(earlier.astype(jnp.int32), axis=1)
    student_slot = (block_owner * KB_DEV + ordinal).astype(jnp.int32)
    return jnp.zeros((NB,), jnp.int32).at[student_slot].set(numbers)


def reference(teacher_logits, student_hidden, student_head, keep_ids, block_owner, block_count):
    slot_block = student_layout(block_owner)
    lane_index = jnp.arange(BLOCK, dtype=jnp.int32)
    valid_cols = (lane_index[None, :] < block_count[slot_block][:, None]).reshape(KEPT)
    kept_ids = keep_ids[slot_block].reshape(KEPT)
    safe_ids = jnp.where(valid_cols, kept_ids, 0).astype(jnp.int32)
    row_block = math.gcd(TOKENS, 128)
    blocks_count = TOKENS // row_block

    def one_block(inputs):
        logit_rows, hidden_rows = inputs
        values = logit_rows.astype(jnp.float32)
        top_logit = jnp.max(values, axis=1, keepdims=True)
        exp_total = jnp.sum(jnp.exp(values - top_logit), axis=1, keepdims=True)
        picked = jnp.take(logit_rows, safe_ids, axis=1).astype(jnp.float32)
        kept = jnp.where(valid_cols[None, :], jnp.exp(picked - top_logit) / exp_total, 0.0).astype(jnp.bfloat16)
        scores = jnp.dot(hidden_rows, student_head, preferred_element_type=jnp.float32)
        masked = jnp.where(valid_cols[None, :], scores, -jnp.inf)
        student_top = jnp.max(masked, axis=1, keepdims=True)
        weight = jnp.where(valid_cols[None, :], jnp.exp(masked - student_top), 0.0)
        exp_norm = jnp.sum(weight, axis=1, keepdims=True)
        kept_mass = jnp.sum(kept.astype(jnp.float32), axis=1, keepdims=True)
        gradient = loss_scale * ((weight / exp_norm) * kept_mass - kept.astype(jnp.float32))
        return gradient.astype(jnp.bfloat16)

    logit_grads = lax.map(one_block, (teacher_logits.reshape(blocks_count, row_block, VOCAB),
                                      student_hidden.reshape(blocks_count, row_block, D)))
    logit_grads = logit_grads.reshape(TOKENS, KEPT)
    head_grad = lax.dot_general(student_hidden, logit_grads, (((0,), (0,)), ((), ())),
                                preferred_element_type=jnp.float32).astype(jnp.bfloat16)
    hidden_grad = lax.dot_general(logit_grads, student_head, (((1,), (1,)), ((), ())),
                                  preferred_element_type=jnp.float32).astype(jnp.bfloat16)
    return head_grad, hidden_grad
```

```python
import jax
import jax.numpy as jnp
from jax import lax
from jax.sharding import PartitionSpec as P

loss_scale = 8192.0


def exchange(value, axes):
    count = lax.axis_size(axes)
    copies = jnp.broadcast_to(value[None], (count,) + value.shape)
    return lax.all_to_all(copies, axes, split_axis=0, concat_axis=0, tiled=True)


def line_gather(value, axis):
    size = lax.axis_size(axis)
    ups, downs = [], []
    rising = falling = value
    for step in range(size - 1):
        rising = lax.ppermute(rising, axis, [(p, p + 1) for p in range(step, size - 1)])
        falling = lax.ppermute(falling, axis, [(p + 1, p) for p in range(size - 1 - step)])
        ups.append(rising)
        downs.append(falling)
    return [ups[k - 1] + downs[size - k - 1] for k in range(1, size)]


def halving_sum(value, axis):
    size = lax.axis_size(axis)
    index = lax.axis_index(axis)
    tail = value.shape[1:]
    groups = 1
    bit = 1
    while bit < size:
        pairs = [(i, i ^ bit) for i in range(size)]
        split = value.reshape((size // (2 * bit), 2, 1) + tail)
        mine = (index // bit) % 2
        keep = lax.dynamic_index_in_dim(split, mine, 1, keepdims=False)
        send = lax.dynamic_index_in_dim(split, 1 - mine, 1, keepdims=False)
        value = (keep + lax.ppermute(send, axis, pairs)).reshape((size // (2 * bit),) + tail)
        bit *= 2
    return value[0]


def shards(teacher_logits, student_hidden, student_head, keep_ids, block_owner, block_count):
    planes = lax.axis_size("dp")
    plane = lax.axis_index("dp")
    shard_count = lax.axis_size("vocab")
    my_shard = lax.axis_index("vocab")
    tok_rows, vocab_rows = teacher_logits.shape
    slab, own_cols = student_head.shape
    width = student_hidden.shape[1]
    lane_count = keep_ids.shape[1]
    kept_blocks = block_owner.shape[0] // shard_count
    part_blocks = kept_blocks // planes
    part_cols = own_cols // planes
    slice_rows = tok_rows // shard_count
    tokens = planes * tok_rows
    capacity = (2 * kept_blocks + shard_count - 1) // shard_count

    head = lax.all_to_all(
        student_head.reshape(slab, planes, part_cols).transpose(1, 0, 2),
        "dp", split_axis=0, concat_axis=0, tiled=True,
    ).reshape(width, part_cols)

    numbers = jnp.arange(block_owner.shape[0], dtype=jnp.int32)
    lane_index = jnp.arange(lane_count, dtype=jnp.int32)
    source = keep_ids[:, 0] // vocab_rows
    owner_before = (block_owner[None, :] == block_owner[:, None]) & (
        numbers[None, :] < numbers[:, None]
    )
    ordinal = jnp.sum(owner_before.astype(jnp.int32), axis=1)
    pair_rank = jnp.sum(
        (owner_before & (source[None, :] == source[:, None])).astype(jnp.int32), axis=1
    )
    send_slots = jnp.arange(shard_count * capacity, dtype=jnp.int32)
    outgoing = (
        (source == my_shard)[None, :]
        & (block_owner[None, :] == (send_slots // capacity)[:, None])
        & (pair_rank[None, :] == (send_slots % capacity)[:, None])
    )
    present = jnp.any(outgoing, axis=1)
    chosen = jnp.sum(jnp.where(outgoing, numbers[None, :], 0), axis=1)
    live_slots = present[:, None] & (lane_index[None, :] < block_count[chosen][:, None])
    columns = jnp.where(live_slots, keep_ids[chosen] - my_shard * vocab_rows, 0).reshape(-1)

    picked = jnp.take(teacher_logits, columns, axis=1)
    arrived = lax.all_to_all(
        picked.reshape(tok_rows, shard_count * capacity, lane_count).transpose(1, 0, 2),
        "vocab", split_axis=0, concat_axis=0, tiled=True,
    )
    incoming = (block_owner[None, :] == my_shard) & (
        ordinal[None, :] == jnp.arange(kept_blocks, dtype=jnp.int32)[:, None]
    )
    own_blocks = jnp.sum(jnp.where(incoming, numbers[None, :], 0), axis=1)
    anchor = source[own_blocks] * capacity + pair_rank[own_blocks]
    target = lax.all_to_all(
        jnp.take(arrived, anchor, axis=0), "dp", split_axis=0, concat_axis=0, tiled=True
    )
    target = (
        target.reshape(planes, part_blocks, tok_rows, lane_count)
        .transpose(0, 2, 1, 3)
        .reshape(tokens, part_cols)
        .astype(jnp.float32)
    )
    own_counts = block_count[lax.dynamic_slice_in_dim(own_blocks, plane * part_blocks, part_blocks)]
    valid_cols = (lane_index[None, :] < own_counts[:, None]).reshape(-1)[None, :]

    hidden_slice = lax.dynamic_slice_in_dim(student_hidden, my_shard * slice_rows, slice_rows)
    hidden = exchange(exchange(hidden_slice, "dp"), "vocab")
    hidden = (
        hidden.reshape(shard_count, planes, slice_rows, width)
        .transpose(1, 0, 2, 3)
        .reshape(tokens, width)
    )

    values = teacher_logits.astype(jnp.float32)
    local_peak = jnp.max(values, axis=1)
    local_total = jnp.sum(jnp.exp(values - local_peak[:, None]), axis=1)
    stats = exchange(jnp.stack([local_peak, local_total]), ("dp", "vocab"))
    stats = stats.reshape(planes, shard_count, 2, tok_rows)
    peak = jnp.max(stats[:, :, 0], axis=1)
    total = jnp.sum(stats[:, :, 1] * jnp.exp(stats[:, :, 0] - peak[:, None]), axis=1)
    kept = jnp.where(
        valid_cols, jnp.exp(target - peak.reshape(-1, 1)) / total.reshape(-1, 1), 0.0
    ).astype(jnp.bfloat16).astype(jnp.float32)

    scores = jnp.dot(hidden, head, preferred_element_type=jnp.float32)
    masked = jnp.where(valid_cols, scores, -jnp.inf)
    local_top = jnp.max(masked, axis=1)
    weight = jnp.where(valid_cols, jnp.exp(masked - local_top[:, None]), 0.0)
    student = exchange(
        jnp.stack([local_top, jnp.sum(weight, axis=1), jnp.sum(kept, axis=1)]), ("dp", "vocab")
    ).reshape(planes * shard_count, 3, tokens)
    student_top = jnp.max(student[:, 0], axis=0)
    exp_norm = jnp.sum(student[:, 1] * jnp.exp(student[:, 0] - student_top), axis=0)
    kept_mass = jnp.sum(student[:, 2], axis=0)
    factor = jnp.exp(local_top - student_top) / exp_norm * kept_mass
    gradient = (loss_scale * (weight * factor[:, None] - kept)).astype(jnp.bfloat16)

    partial_sums = lax.dot_general(
        gradient, head, (((1,), (1,)), ((), ())), preferred_element_type=jnp.float32
    )
    partial_sums = (
        partial_sums.reshape(planes, shard_count, slice_rows, width).transpose(1, 0, 2, 3)
    )
    partial_sums = halving_sum(partial_sums, "vocab")
    partial_sums = lax.all_to_all(partial_sums, "dp", split_axis=0, concat_axis=0, tiled=True)
    hidden_grad = jnp.sum(partial_sums.reshape(planes, slice_rows, width), axis=0)

    own_hidden = lax.dynamic_slice_in_dim(hidden, plane * slab, slab, axis=1)
    head_grad = jnp.zeros((slab, own_cols), jnp.bfloat16)
    for distance, columns_part in enumerate([gradient] + line_gather(gradient, "dp")):
        origin = lax.rem(plane + planes - distance, planes)
        block = lax.dot_general(
            own_hidden, columns_part, (((0,), (0,)), ((), ())), preferred_element_type=jnp.float32
        ).astype(jnp.bfloat16)
        head_grad = lax.dynamic_update_slice_in_dim(head_grad, block, origin * part_cols, axis=1)
    return (head_grad, hidden_grad.astype(jnp.bfloat16))


def solution(mesh):
    return jax.shard_map(
        shards,
        mesh=mesh,
        in_specs=(P("dp", "vocab"), P("dp", None), P("dp", "vocab"), P(), P(), P()),
        out_specs=(P("dp", "vocab"), P(("dp", "vocab"), None)),
        check_vma=False,
    )
```

```python
import jax
import jax.numpy as jnp
from jax import lax
from jax.sharding import PartitionSpec as P


loss_scale = 8192.0


def exchange(value, axes):
    count = lax.axis_size(axes)
    copies = jnp.broadcast_to(value[None], (count,) + value.shape)
    return lax.all_to_all(copies, axes, split_axis=0, concat_axis=0, tiled=True)


def shift(value, axis, distance):
    size = lax.axis_size(axis)
    return lax.ppermute(value, axis, [(p, (p + distance) % size) for p in range(size)])


def above(axis, distance):
    size = lax.axis_size(axis)
    return lax.rem(lax.axis_index(axis) + size + distance, size)


def spread(value, axis):
    size = lax.axis_size(axis)
    index = lax.axis_index(axis)
    if size != 4:
        return [(above(axis, -d), shift(value, axis, d)) for d in range(1, size)]
    middle = shift(value, axis, 2)
    rising = lax.ppermute(value, axis, [(p, p + 1) for p in range(size - 1)])
    falling = lax.ppermute(value, axis, [(p + 1, p) for p in range(size - 1)])
    relay = lax.ppermute(middle, axis, [(1, 0), (2, 3)])
    first, last = index == 0, index == size - 1
    near = jnp.where(first, falling, rising)
    far = jnp.where(first | last, relay, falling)
    return [
        (jnp.where(first, 1, index - 1), near),
        (lax.rem(index + 2, size), middle),
        (jnp.where(first, size - 1, jnp.where(last, 0, index + 1)), far),
    ]


def direct_sum(part, axis):
    size = lax.axis_size(axis)
    index = lax.axis_index(axis)
    far = lax.ppermute(part(1 - index % 2), axis, [(i, i ^ 1) for i in range(size)])
    value = part(index % 2) + far
    total = lax.dynamic_index_in_dim(value, index // 2, 0, keepdims=False)
    for step in range(1, size // 2):
        send = lax.dynamic_index_in_dim(value, (index // 2) ^ step, 0, keepdims=False)
        send = lax.ppermute(send, axis, [(i, i ^ (2 * step)) for i in range(size)])
        total = total + send
    return total


def in_order(pieces, axis):
    size = len(pieces)
    order = lax.rem(lax.axis_index(axis) + size - jnp.arange(size, dtype=jnp.int32), size)
    return jnp.take(jnp.stack(pieces), order, axis=0, mode="clip")


def shards(teacher_logits, student_hidden, student_head, keep_ids, block_owner, block_count):
    planes = lax.axis_size("dp")
    plane = lax.axis_index("dp")
    shard_count = lax.axis_size("vocab")
    my_shard = lax.axis_index("vocab")
    tok_rows, vocab_rows = teacher_logits.shape
    slab, own_cols = student_head.shape
    width = student_hidden.shape[1]
    lane_count = keep_ids.shape[1]
    kept_blocks = block_owner.shape[0] // shard_count
    part_blocks = kept_blocks // planes
    part_cols = own_cols // planes
    slice_rows = tok_rows // shard_count
    tokens = planes * tok_rows
    capacity = (2 * kept_blocks + shard_count - 1) // shard_count

    pieces = []
    for distance in range(planes):
        piece = lax.dynamic_slice_in_dim(
            student_head, above("dp", distance) * part_cols, part_cols, 1
        )
        pieces.append(shift(piece, "dp", distance) if distance else piece)

    hidden_slice = lax.dynamic_slice_in_dim(student_hidden, my_shard * slice_rows, slice_rows)
    hidden = [shift(hidden_slice, "dp", d) if d else hidden_slice for d in range(planes)]
    hidden = in_order(hidden, "dp")
    hidden = exchange(hidden, "vocab").reshape(tokens, width)

    numbers = jnp.arange(block_owner.shape[0], dtype=jnp.int32)
    lane_index = jnp.arange(lane_count, dtype=jnp.int32)
    source = keep_ids[:, 0] // vocab_rows
    owner_before = (block_owner[None, :] == block_owner[:, None]) & (
        numbers[None, :] < numbers[:, None]
    )
    ordinal = jnp.sum(owner_before.astype(jnp.int32), axis=1)
    pair_rank = jnp.sum(
        (owner_before & (source[None, :] == source[:, None])).astype(jnp.int32), axis=1
    )
    send_slots = jnp.arange(shard_count * capacity, dtype=jnp.int32)
    outgoing = (
        (source == my_shard)[None, :]
        & (block_owner[None, :] == (send_slots // capacity)[:, None])
        & (pair_rank[None, :] == (send_slots % capacity)[:, None])
    )
    chosen = jnp.sum(jnp.where(outgoing, numbers[None, :], 0), axis=1)
    columns = jnp.clip(keep_ids[chosen] - my_shard * vocab_rows, 0, vocab_rows - 1).reshape(-1)
    incoming = (block_owner[None, :] == my_shard) & (
        ordinal[None, :] == jnp.arange(kept_blocks, dtype=jnp.int32)[:, None]
    )
    own_blocks = jnp.sum(jnp.where(incoming, numbers[None, :], 0), axis=1)
    anchor = source[own_blocks] * (capacity + 1) + pair_rank[own_blocks]
    valid = lane_index[None, :] < block_count[own_blocks][:, None]

    values = teacher_logits.astype(jnp.float32)
    local_peak = jnp.max(values, axis=1)
    local_total = jnp.sum(jnp.exp(values - local_peak[:, None]), axis=1)
    terms = [local_peak]
    for _ in range(3):
        terms.append(lax.reduce_precision(local_total, 8, 7))
        local_total = local_total - terms[-1]
    terms = jnp.stack(terms, axis=1).astype(jnp.bfloat16)
    terms = jnp.pad(terms, ((0, 0), (0, lane_count - terms.shape[1])))

    picked = jnp.take(teacher_logits, columns, axis=1, mode="clip")
    picked = picked.reshape(tok_rows, shard_count, capacity, lane_count).transpose(1, 2, 0, 3)
    terms = jnp.broadcast_to(terms, (shard_count, 1, tok_rows, lane_count))
    picked = jnp.concatenate([picked, terms], axis=1)
    hidden, picked = lax.optimization_barrier((hidden, picked))
    arrived = lax.all_to_all(picked, "vocab", split_axis=0, concat_axis=0, tiled=True)
    stats = arrived[:, capacity, :, :4].astype(jnp.float32)
    totals = stats[:, :, 1] + stats[:, :, 2] + stats[:, :, 3]
    peak = jnp.max(stats[:, :, 0], axis=0)
    total = jnp.sum(totals * jnp.exp(stats[:, :, 0] - peak), axis=0)

    arrived = arrived.reshape(shard_count * (capacity + 1), tok_rows, lane_count)
    target = jnp.take(arrived, anchor, axis=0, mode="clip").astype(jnp.float32)
    target = jnp.where(
        valid[:, None, :], jnp.exp(target - peak[None, :, None]) / total[None, :, None], 0.0
    ).astype(jnp.bfloat16)
    mass_part = jnp.sum(target.astype(jnp.float32), axis=(0, 2))

    target = target.reshape(planes, part_blocks, tok_rows, lane_count)
    kept = []
    for distance in range(planes):
        piece = lax.dynamic_index_in_dim(target, above("dp", distance), 0, keepdims=False)
        kept.append(shift(piece, "dp", distance) if distance else piece)
    valid_cols = lax.dynamic_slice_in_dim(valid, plane * part_blocks, part_blocks).reshape(1, -1)

    scores = sum(
        jnp.dot(
            lax.dynamic_slice_in_dim(hidden, above("dp", -distance) * slab, slab, axis=1),
            piece, preferred_element_type=jnp.float32,
        )
        for distance, piece in enumerate(pieces)
    )
    masked = jnp.where(valid_cols, scores, -jnp.inf)
    local_top = jnp.max(masked, axis=1)
    weight = jnp.where(valid_cols, jnp.exp(masked - local_top[:, None]), 0.0)
    student = jnp.concatenate([local_top, jnp.sum(weight, axis=1), mass_part])
    pieces, kept, student = lax.optimization_barrier((pieces, kept, student))
    kept = in_order(kept, "dp").reshape(
        planes, part_blocks, shard_count, slice_rows, lane_count
    ).transpose(2, 0, 3, 1, 4).reshape(tokens, part_cols).astype(jnp.float32)
    student = exchange(student.reshape(-1, tok_rows), ("dp", "vocab")).reshape(
        planes * shard_count, 2 * planes + 1, tok_rows
    )
    tops, norms = student[:, :planes], student[:, planes : 2 * planes]
    student_top = jnp.max(tops, axis=0)
    exp_norm = jnp.sum(norms * jnp.exp(tops - student_top), axis=0)
    kept_mass = jnp.sum(student[:, 2 * planes].reshape(planes, shard_count, tok_rows), axis=1)
    kept_mass = kept_mass.reshape(planes, shard_count, slice_rows).transpose(1, 0, 2).reshape(-1)
    factor = jnp.exp(local_top - student_top.reshape(-1)) / exp_norm.reshape(-1) * kept_mass
    gradient = (loss_scale * (weight * factor[:, None] - kept)).astype(jnp.bfloat16)

    gradients = [(plane, gradient)] + spread(gradient, "dp")

    head = in_order(pieces, "dp").reshape(width, part_cols)
    by_pair = gradient.reshape(shard_count // 2, 2, planes * slice_rows, part_cols)

    def part(last_bit):
        rows = lax.dynamic_index_in_dim(by_pair, last_bit, 1, keepdims=False)
        product = lax.dot_general(
            rows.reshape(-1, part_cols), head, (((1,), (1,)), ((), ())),
            preferred_element_type=jnp.float32,
        )
        return product.reshape(shard_count // 2, planes, slice_rows, width)

    sums = direct_sum(part, "vocab")
    sums = lax.all_to_all(sums, "dp", split_axis=0, concat_axis=0, tiled=True)
    hidden_grad = jnp.sum(sums, axis=0).astype(jnp.bfloat16)

    own_hidden = lax.dynamic_slice_in_dim(hidden, plane * slab, slab, axis=1)
    head_grad = jnp.zeros((slab, own_cols), jnp.bfloat16)
    for origin, columns_part in gradients:
        block = lax.dot_general(
            own_hidden, columns_part, (((0,), (0,)), ((), ())), preferred_element_type=jnp.float32
        ).astype(jnp.bfloat16)
        head_grad = lax.dynamic_update_slice_in_dim(head_grad, block, origin * part_cols, axis=1)
    return (head_grad, hidden_grad)


def solution(mesh):
    return jax.shard_map(
        shards,
        mesh=mesh,
        in_specs=(P("dp", "vocab"), P("dp", None), P("dp", "vocab"), P(), P(), P()),
        out_specs=(P("dp", "vocab"), P(("dp", "vocab"), None)),
        check_vma=False,
    )
```

```python
import functools

import jax
import jax.numpy as jnp
from jax import lax
from jax.experimental import pallas as pl
from jax.experimental.pallas import tpu as pltpu
from jax.sharding import PartitionSpec as P


loss_scale = 8192.0


def exchange(value, axes):
    count = lax.axis_size(axes)
    copies = jnp.broadcast_to(value[None], (count,) + value.shape)
    return lax.all_to_all(copies, axes, split_axis=0, concat_axis=0, tiled=True)


def shift(value, axis, distance):
    size = lax.axis_size(axis)
    return lax.ppermute(value, axis, [(p, (p + distance) % size) for p in range(size)])


def above(axis, distance):
    size = lax.axis_size(axis)
    return lax.rem(lax.axis_index(axis) + size + distance, size)


def chip_gather(value, axis):
    size = lax.axis_size(axis)
    index = lax.axis_index(axis)
    like = [value]
    for step in range(1, size // 2):
        like.append(lax.ppermute(value, axis, [(i, i ^ (2 * step)) for i in range(size)]))
    like = jnp.stack(like)
    other = lax.ppermute(like, axis, [(i, i ^ 1) for i in range(size)])
    both = jnp.stack([like, other], axis=1).reshape((size,) + value.shape)
    order = jnp.bitwise_xor(jnp.arange(size, dtype=jnp.int32), index)
    return jnp.take(both, order, axis=0, mode="clip")


def spread(value, axis):
    size = lax.axis_size(axis)
    index = lax.axis_index(axis)
    if size != 4:
        return [(above(axis, -d), shift(value, axis, d)) for d in range(1, size)]
    middle = shift(value, axis, 2)
    rising = lax.ppermute(value, axis, [(p, p + 1) for p in range(size - 1)])
    falling = lax.ppermute(value, axis, [(p + 1, p) for p in range(size - 1)])
    relay = lax.ppermute(middle, axis, [(1, 0), (2, 3)])
    first, last = index == 0, index == size - 1
    near = jnp.where(first, falling, rising)
    far = jnp.where(first | last, relay, falling)
    return [
        (jnp.where(first, 1, index - 1), near),
        (lax.rem(index + 2, size), middle),
        (jnp.where(first, size - 1, jnp.where(last, 0, index + 1)), far),
    ]


def direct_sum(part, axis):
    size = lax.axis_size(axis)
    index = lax.axis_index(axis)
    far = lax.ppermute(part(1 - index % 2), axis, [(i, i ^ 1) for i in range(size)])
    value = part(index % 2) + far
    total = lax.dynamic_index_in_dim(value, index // 2, 0, keepdims=False)
    for step in range(1, size // 2):
        send = lax.dynamic_index_in_dim(value, (index // 2) ^ step, 0, keepdims=False)
        send = lax.ppermute(send, axis, [(i, i ^ (2 * step)) for i in range(size)])
        total = total + send
    return total


def in_order(pieces, axis):
    size = len(pieces)
    order = lax.rem(lax.axis_index(axis) + size - jnp.arange(size, dtype=jnp.int32), size)
    return jnp.take(jnp.stack(pieces), order, axis=0, mode="clip")


def pick_kernel(capacity, ids_ref, count_ref, logits_ref, out_ref, wide_ref, rows_ref):
    vocab_rows, tok_rows = logits_ref.shape
    lanes = out_ref.shape[2]
    step = next(s for s in (400, 320, 160, 80, 16) if vocab_rows % s == 0)

    def widen(i, peak):
        rows = pl.ds(pl.multiple_of(i * step, step), step)
        part = logits_ref[rows, :].astype(jnp.float32)
        wide_ref[rows, :] = part
        return jnp.maximum(peak, jnp.max(part, axis=0, keepdims=True))

    peak = lax.fori_loop(0, vocab_rows // step, widen, jnp.full((1, tok_rows), -jnp.inf, jnp.float32))

    def add(i, total):
        rows = pl.ds(pl.multiple_of(i * step, step), step)
        return total + jnp.sum(jnp.exp(wide_ref[rows, :] - peak), axis=0, keepdims=True)

    total = lax.fori_loop(0, vocab_rows // step, add, jnp.zeros((1, tok_rows), jnp.float32))
    rows_ref[...] = jnp.zeros_like(rows_ref)
    first = total.astype(jnp.bfloat16).astype(jnp.float32)
    second = (total - first).astype(jnp.bfloat16).astype(jnp.float32)
    rows_ref[0:1, :] = peak
    rows_ref[1:2, :] = first
    rows_ref[2:3, :] = second
    rows_ref[3:4, :] = total - first - second
    terms = rows_ref[...].astype(out_ref.dtype)
    for shard in range(out_ref.shape[0]):
        out_ref[shard, capacity] = terms

    def slot(s, _):
        def eight(g, _):
            for j in range(8):
                row = ids_ref[s * lanes + g * 8 + j]
                rows_ref[pl.ds(g * 8 + j, 1), :] = wide_ref[pl.ds(row, 1), :]
            return 0

        @pl.when(count_ref[s] > 0)
        def _():
            lax.fori_loop(0, (count_ref[s] + 7) // 8, eight, 0)
            out_ref[s // capacity, s % capacity] = rows_ref[...].astype(out_ref.dtype)

        return 0

    lax.fori_loop(0, out_ref.shape[0] * capacity, slot, 0)


def pick(teacher_logits, ids, counts, shards, capacity):
    tok_rows, vocab_rows = teacher_logits.shape
    lanes = ids.shape[1]
    return pl.pallas_call(
        functools.partial(pick_kernel, capacity),
        out_shape=jax.ShapeDtypeStruct(
            (shards, capacity + 1, lanes, tok_rows), teacher_logits.dtype
        ),
        in_specs=[
            pl.BlockSpec(memory_space=pltpu.SMEM),
            pl.BlockSpec(memory_space=pltpu.SMEM),
            pl.BlockSpec(memory_space=pltpu.VMEM),
        ],
        out_specs=pl.BlockSpec(memory_space=pltpu.VMEM),
        scratch_shapes=[
            pltpu.VMEM((vocab_rows, tok_rows), jnp.float32),
            pltpu.VMEM((lanes, tok_rows), jnp.float32),
        ],
    )(ids.reshape(-1), counts, teacher_logits.T)


def kept_kernel(capacity, anchor_ref, count_ref, arrived_ref, kept_ref, mass_ref):
    shards = arrived_ref.shape[0] // (capacity + 1)
    tops, sums = [], []
    for shard in range(shards):
        terms = arrived_ref[shard * (capacity + 1) + capacity, 0:16, :].astype(jnp.float32)
        tops.append(terms[0:1])
        sums.append(terms[1:2] + terms[2:3] + terms[3:4])
    peak = functools.reduce(jnp.maximum, tops)
    total = sum(part * jnp.exp(top - peak) for top, part in zip(tops, sums))
    lane = lax.broadcasted_iota(jnp.int32, kept_ref.shape[1:], 0)

    def block(b, mass):
        logits = arrived_ref[anchor_ref[b]].astype(jnp.float32)
        probs = jnp.where(lane < count_ref[b], jnp.exp(logits - peak) / total, 0.0)
        kept = probs.astype(kept_ref.dtype)
        kept_ref[b] = kept
        return mass + jnp.sum(kept.astype(jnp.float32), axis=0, keepdims=True)

    mass_ref[...] = lax.fori_loop(0, kept_ref.shape[0], block, jnp.zeros(mass_ref.shape, jnp.float32))


def kept_probabilities(arrived, anchor, counts, capacity):
    lanes, tok_rows = arrived.shape[2:]
    return pl.pallas_call(
        functools.partial(kept_kernel, capacity),
        out_shape=(
            jax.ShapeDtypeStruct((anchor.shape[0], lanes, tok_rows), arrived.dtype),
            jax.ShapeDtypeStruct((1, tok_rows), jnp.float32),
        ),
        in_specs=[
            pl.BlockSpec(memory_space=pltpu.SMEM),
            pl.BlockSpec(memory_space=pltpu.SMEM),
            pl.BlockSpec(memory_space=pltpu.VMEM),
        ],
        out_specs=[pl.BlockSpec(memory_space=pltpu.VMEM)] * 2,
    )(anchor, counts, arrived.reshape(-1, lanes, tok_rows))


def shards(teacher_logits, student_hidden, student_head, keep_ids, block_owner, block_count):
    planes = lax.axis_size("dp")
    plane = lax.axis_index("dp")
    shard_count = lax.axis_size("vocab")
    my_shard = lax.axis_index("vocab")
    tok_rows, vocab_rows = teacher_logits.shape
    slab, own_cols = student_head.shape
    width = student_hidden.shape[1]
    lane_count = keep_ids.shape[1]
    kept_blocks = block_owner.shape[0] // shard_count
    part_blocks = kept_blocks // planes
    part_cols = own_cols // planes
    slice_rows = tok_rows // shard_count
    tokens = planes * tok_rows
    capacity = (2 * kept_blocks + shard_count - 1) // shard_count

    pieces = []
    for distance in range(planes):
        piece = lax.dynamic_slice_in_dim(
            student_head, above("dp", distance) * part_cols, part_cols, 1
        )
        pieces.append(shift(piece, "dp", distance) if distance else piece)

    hidden_slice = lax.dynamic_slice_in_dim(student_hidden, my_shard * slice_rows, slice_rows)
    hidden = [shift(hidden_slice, "dp", d) if d else hidden_slice for d in range(planes)]
    hidden = chip_gather(in_order(hidden, "dp"), "vocab").reshape(tokens, width)

    numbers = jnp.arange(block_owner.shape[0], dtype=jnp.int32)
    lane_index = jnp.arange(lane_count, dtype=jnp.int32)
    source = keep_ids[:, 0] // vocab_rows
    owner_before = (block_owner[None, :] == block_owner[:, None]) & (
        numbers[None, :] < numbers[:, None]
    )
    ordinal = jnp.sum(owner_before.astype(jnp.int32), axis=1)
    pair_rank = jnp.sum(
        (owner_before & (source[None, :] == source[:, None])).astype(jnp.int32), axis=1
    )
    send_slots = jnp.arange(shard_count * capacity, dtype=jnp.int32)
    outgoing = (
        (source == my_shard)[None, :]
        & (block_owner[None, :] == (send_slots // capacity)[:, None])
        & (pair_rank[None, :] == (send_slots % capacity)[:, None])
    )
    chosen = jnp.sum(jnp.where(outgoing, numbers[None, :], 0), axis=1)
    columns = jnp.clip(keep_ids[chosen] - my_shard * vocab_rows, 0, vocab_rows - 1)
    slot_counts = jnp.sum(jnp.where(outgoing, block_count[None, :], 0), axis=1)
    incoming = (block_owner[None, :] == my_shard) & (
        ordinal[None, :] == jnp.arange(kept_blocks, dtype=jnp.int32)[:, None]
    )
    own_blocks = jnp.sum(jnp.where(incoming, numbers[None, :], 0), axis=1)
    anchor = source[own_blocks] * (capacity + 1) + pair_rank[own_blocks]
    own_counts = block_count[own_blocks]
    valid = lane_index[None, :] < own_counts[:, None]

    picked = pick(teacher_logits, columns, slot_counts, shard_count, capacity)
    arrived = lax.all_to_all(picked, "vocab", split_axis=0, concat_axis=0, tiled=True)
    arrived, hidden = lax.optimization_barrier((arrived, hidden))
    target, mass_part = kept_probabilities(arrived, anchor, own_counts, capacity)
    mass_part = mass_part.reshape(-1)

    target = target.reshape(planes, part_blocks, lane_count, tok_rows)
    kept = []
    for distance in range(planes):
        piece = lax.dynamic_index_in_dim(target, above("dp", distance), 0, keepdims=False)
        kept.append(shift(piece, "dp", distance) if distance else piece)
    valid_cols = lax.dynamic_slice_in_dim(valid, plane * part_blocks, part_blocks).reshape(1, -1)

    scores = sum(
        jnp.dot(
            lax.dynamic_slice_in_dim(hidden, above("dp", -distance) * slab, slab, axis=1),
            piece, preferred_element_type=jnp.float32,
        )
        for distance, piece in enumerate(pieces)
    )
    masked = jnp.where(valid_cols, scores, -jnp.inf)
    local_top = jnp.max(masked, axis=1)
    weight = jnp.where(valid_cols, jnp.exp(masked - local_top[:, None]), 0.0)
    student = jnp.concatenate([local_top, jnp.sum(weight, axis=1), mass_part])
    pieces, kept, student = lax.optimization_barrier((pieces, kept, student))
    kept = in_order(kept, "dp").reshape(
        planes, part_cols, tok_rows
    ).transpose(0, 2, 1).reshape(planes, shard_count, slice_rows, part_cols)
    kept = kept.transpose(1, 0, 2, 3).reshape(tokens, part_cols).astype(jnp.float32)
    student = exchange(student.reshape(-1, tok_rows), ("dp", "vocab")).reshape(
        planes * shard_count, 2 * planes + 1, tok_rows
    )
    tops, norms = student[:, :planes], student[:, planes : 2 * planes]
    student_top = jnp.max(tops, axis=0)
    exp_norm = jnp.sum(norms * jnp.exp(tops - student_top), axis=0)
    kept_mass = jnp.sum(student[:, 2 * planes].reshape(planes, shard_count, tok_rows), axis=1)
    kept_mass = kept_mass.reshape(planes, shard_count, slice_rows).transpose(1, 0, 2).reshape(-1)
    factor = jnp.exp(local_top - student_top.reshape(-1)) / exp_norm.reshape(-1) * kept_mass
    gradient = (loss_scale * (weight * factor[:, None] - kept)).astype(jnp.bfloat16)

    gradients = [(plane, gradient)] + spread(gradient, "dp")

    head = in_order(pieces, "dp").reshape(width, part_cols)
    by_pair = gradient.reshape(shard_count // 2, 2, planes * slice_rows, part_cols)

    def part(last_bit):
        rows = lax.dynamic_index_in_dim(by_pair, last_bit, 1, keepdims=False)
        product = lax.dot_general(
            rows.reshape(-1, part_cols), head, (((1,), (1,)), ((), ())),
            preferred_element_type=jnp.float32,
        )
        return product.reshape(shard_count // 2, planes, slice_rows, width)

    sums = direct_sum(part, "vocab")
    sums = lax.all_to_all(sums, "dp", split_axis=0, concat_axis=0, tiled=True)
    hidden_grad = jnp.sum(sums, axis=0).astype(jnp.bfloat16)

    own_hidden = lax.dynamic_slice_in_dim(hidden, plane * slab, slab, axis=1)
    head_grad = jnp.zeros((slab, own_cols), jnp.bfloat16)
    for origin, columns_part in gradients:
        block = lax.dot_general(
            own_hidden, columns_part, (((0,), (0,)), ((), ())),
            preferred_element_type=jnp.float32,
        ).astype(jnp.bfloat16)
        head_grad = lax.dynamic_update_slice_in_dim(head_grad, block, origin * part_cols, axis=1)
    return (head_grad, hidden_grad)


def solution(mesh):
    return jax.shard_map(
        shards,
        mesh=mesh,
        in_specs=(P("dp", "vocab"), P("dp", None), P("dp", "vocab"), P(), P(), P()),
        out_specs=(P("dp", "vocab"), P(("dp", "vocab"), None)),
        check_vma=False,
    )
```

```python
import functools

import jax
import jax.numpy as jnp
from jax import lax
from jax.experimental import pallas as pl
from jax.experimental.pallas import tpu as pltpu
from jax.sharding import PartitionSpec as P


loss_scale = 8192.0


def exchange(value, axes):
    count = lax.axis_size(axes)
    copies = jnp.broadcast_to(value[None], (count,) + value.shape)
    return lax.all_to_all(copies, axes, split_axis=0, concat_axis=0, tiled=True)


def shift(value, axis, distance):
    size = lax.axis_size(axis)
    return lax.ppermute(value, axis, [(p, (p + distance) % size) for p in range(size)])


def above(axis, distance):
    size = lax.axis_size(axis)
    return lax.rem(lax.axis_index(axis) + size + distance, size)


def chip_gather(value, axis):
    size = lax.axis_size(axis)
    index = lax.axis_index(axis)
    like = [value]
    for step in range(1, size // 2):
        like.append(lax.ppermute(value, axis, [(i, i ^ (2 * step)) for i in range(size)]))
    like = jnp.stack(like)
    other = lax.ppermute(like, axis, [(i, i ^ 1) for i in range(size)])
    both = jnp.stack([like, other], axis=1).reshape((size,) + value.shape)
    order = jnp.bitwise_xor(jnp.arange(size, dtype=jnp.int32), index)
    return jnp.take(both, order, axis=0, mode="clip")


def spread(value, axis):
    size = lax.axis_size(axis)
    index = lax.axis_index(axis)
    if size != 4:
        return [(above(axis, -d), shift(value, axis, d)) for d in range(1, size)]
    middle = shift(value, axis, 2)
    rising = lax.ppermute(value, axis, [(p, p + 1) for p in range(size - 1)])
    falling = lax.ppermute(value, axis, [(p + 1, p) for p in range(size - 1)])
    relay = lax.ppermute(middle, axis, [(1, 0), (2, 3)])
    first, last = index == 0, index == size - 1
    near = jnp.where(first, falling, rising)
    far = jnp.where(first | last, relay, falling)
    return [
        (jnp.where(first, 1, index - 1), near),
        (lax.rem(index + 2, size), middle),
        (jnp.where(first, size - 1, jnp.where(last, 0, index + 1)), far),
    ]


def direct_sum(part, axis):
    size = lax.axis_size(axis)
    index = lax.axis_index(axis)
    far = lax.ppermute(part(1 - index % 2), axis, [(i, i ^ 1) for i in range(size)])
    value = part(index % 2) + far
    total = lax.dynamic_index_in_dim(value, index // 2, 0, keepdims=False)
    for step in range(1, size // 2):
        send = lax.dynamic_index_in_dim(value, (index // 2) ^ step, 0, keepdims=False)
        send = lax.ppermute(send, axis, [(i, i ^ (2 * step)) for i in range(size)])
        total = total + send
    return total


def in_order(pieces, axis):
    size = len(pieces)
    order = lax.rem(lax.axis_index(axis) + size - jnp.arange(size, dtype=jnp.int32), size)
    return jnp.take(jnp.stack(pieces), order, axis=0, mode="clip")


def pick_kernel(capacity, ids_ref, count_ref, logits_ref, out_ref, wide_ref, rows_ref):
    vocab_rows, tok_rows = logits_ref.shape
    lanes = out_ref.shape[2]
    step = next(s for s in (400, 320, 160, 80, 16) if vocab_rows % s == 0)

    def widen(i, peak):
        rows = pl.ds(pl.multiple_of(i * step, step), step)
        part = logits_ref[rows, :].astype(jnp.float32)
        wide_ref[rows, :] = part
        return jnp.maximum(peak, jnp.max(part, axis=0, keepdims=True))

    peak = lax.fori_loop(0, vocab_rows // step, widen, jnp.full((1, tok_rows), -jnp.inf, jnp.float32))

    def add(i, total):
        rows = pl.ds(pl.multiple_of(i * step, step), step)
        return total + jnp.sum(jnp.exp(wide_ref[rows, :] - peak), axis=0, keepdims=True)

    total = lax.fori_loop(0, vocab_rows // step, add, jnp.zeros((1, tok_rows), jnp.float32))
    rows_ref[...] = jnp.zeros_like(rows_ref)
    first = total.astype(jnp.bfloat16).astype(jnp.float32)
    second = (total - first).astype(jnp.bfloat16).astype(jnp.float32)
    rows_ref[0:1, :] = peak
    rows_ref[1:2, :] = first
    rows_ref[2:3, :] = second
    rows_ref[3:4, :] = total - first - second
    terms = rows_ref[...].astype(out_ref.dtype)
    for shard in range(out_ref.shape[0]):
        out_ref[shard, capacity] = terms

    def slot(s, _):
        def eight(g, _):
            for j in range(8):
                row = ids_ref[s * lanes + g * 8 + j]
                rows_ref[pl.ds(g * 8 + j, 1), :] = wide_ref[pl.ds(row, 1), :]
            return 0

        @pl.when(count_ref[s] > 0)
        def _():
            lax.fori_loop(0, (count_ref[s] + 7) // 8, eight, 0)
            out_ref[s // capacity, s % capacity] = rows_ref[...].astype(out_ref.dtype)

        return 0

    lax.fori_loop(0, out_ref.shape[0] * capacity, slot, 0)


def pick(teacher_logits, ids, counts, shards, capacity):
    tok_rows, vocab_rows = teacher_logits.shape
    lanes = ids.shape[1]
    return pl.pallas_call(
        functools.partial(pick_kernel, capacity),
        out_shape=jax.ShapeDtypeStruct(
            (shards, capacity + 1, lanes, tok_rows), teacher_logits.dtype
        ),
        in_specs=[
            pl.BlockSpec(memory_space=pltpu.SMEM),
            pl.BlockSpec(memory_space=pltpu.SMEM),
            pl.BlockSpec(memory_space=pltpu.VMEM),
        ],
        out_specs=pl.BlockSpec(memory_space=pltpu.VMEM),
        scratch_shapes=[
            pltpu.VMEM((vocab_rows, tok_rows), jnp.float32),
            pltpu.VMEM((lanes, tok_rows), jnp.float32),
        ],
    )(ids.reshape(-1), counts, teacher_logits.T)


def kept_kernel(capacity, anchor_ref, count_ref, arrived_ref, kept_ref, mass_ref):
    shards = arrived_ref.shape[0] // (capacity + 1)
    tops, sums = [], []
    for shard in range(shards):
        terms = arrived_ref[shard * (capacity + 1) + capacity, 0:16, :].astype(jnp.float32)
        tops.append(terms[0:1])
        sums.append(terms[1:2] + terms[2:3] + terms[3:4])
    peak = functools.reduce(jnp.maximum, tops)
    total = sum(part * jnp.exp(top - peak) for top, part in zip(tops, sums))
    lane = lax.broadcasted_iota(jnp.int32, kept_ref.shape[1:], 0)

    def block(b, mass):
        logits = arrived_ref[anchor_ref[b]].astype(jnp.float32)
        probs = jnp.where(lane < count_ref[b], jnp.exp(logits - peak) / total, 0.0)
        kept = probs.astype(kept_ref.dtype)
        kept_ref[b] = kept
        return mass + jnp.sum(kept.astype(jnp.float32), axis=0, keepdims=True)

    mass_ref[...] = lax.fori_loop(0, kept_ref.shape[0], block, jnp.zeros(mass_ref.shape, jnp.float32))


def kept_probabilities(arrived, anchor, counts, capacity):
    lanes, tok_rows = arrived.shape[2:]
    return pl.pallas_call(
        functools.partial(kept_kernel, capacity),
        out_shape=(
            jax.ShapeDtypeStruct((anchor.shape[0], lanes, tok_rows), arrived.dtype),
            jax.ShapeDtypeStruct((1, tok_rows), jnp.float32),
        ),
        in_specs=[
            pl.BlockSpec(memory_space=pltpu.SMEM),
            pl.BlockSpec(memory_space=pltpu.SMEM),
            pl.BlockSpec(memory_space=pltpu.VMEM),
        ],
        out_specs=[pl.BlockSpec(memory_space=pltpu.VMEM)] * 2,
    )(anchor, counts, arrived.reshape(-1, lanes, tok_rows))


def place_kernel(planes, origin_ref, *refs):
    heads, kepts, (head_ref, kept_ref) = refs[:planes], refs[planes : 2 * planes], refs[2 * planes :]
    shards, _, rows, _ = kept_ref.shape
    for distance in range(planes):
        origin = origin_ref[distance]
        slab, _ = heads[distance].shape
        head_ref[pl.ds(pl.multiple_of(origin * slab, 16), slab), :] = heads[distance][...]
        blocks, lanes, _ = kepts[distance].shape
        for block in range(blocks):
            tile = kepts[distance][block].astype(jnp.float32).T
            for shard in range(shards):
                kept_ref[shard, pl.ds(origin, 1), :, block * lanes : (block + 1) * lanes] = tile[
                    None, shard * rows : (shard + 1) * rows
                ]


def place(origins, heads, kepts, shards):
    planes = len(heads)
    slab, part_cols = heads[0].shape
    rows = kepts[0].shape[2] // shards
    vmem = pl.BlockSpec(memory_space=pltpu.VMEM)
    return pl.pallas_call(
        functools.partial(place_kernel, planes),
        out_shape=(
            jax.ShapeDtypeStruct((planes * slab, part_cols), heads[0].dtype),
            jax.ShapeDtypeStruct((shards, planes, rows, part_cols), jnp.float32),
        ),
        in_specs=[pl.BlockSpec(memory_space=pltpu.SMEM)] + [vmem] * (2 * planes),
        out_specs=[vmem] * 2,
    )(origins, *heads, *kepts)


def shards(teacher_logits, student_hidden, student_head, keep_ids, block_owner, block_count):
    planes = lax.axis_size("dp")
    plane = lax.axis_index("dp")
    shard_count = lax.axis_size("vocab")
    my_shard = lax.axis_index("vocab")
    tok_rows, vocab_rows = teacher_logits.shape
    slab, own_cols = student_head.shape
    width = student_hidden.shape[1]
    lane_count = keep_ids.shape[1]
    kept_blocks = block_owner.shape[0] // shard_count
    part_blocks = kept_blocks // planes
    part_cols = own_cols // planes
    slice_rows = tok_rows // shard_count
    tokens = planes * tok_rows
    capacity = (2 * kept_blocks + shard_count - 1) // shard_count

    pieces = []
    for distance in range(planes):
        piece = lax.dynamic_slice_in_dim(
            student_head, above("dp", distance) * part_cols, part_cols, 1
        )
        pieces.append(shift(piece, "dp", distance) if distance else piece)

    hidden_slice = lax.dynamic_slice_in_dim(student_hidden, my_shard * slice_rows, slice_rows)
    hidden = [shift(hidden_slice, "dp", d) if d else hidden_slice for d in range(planes)]
    hidden = chip_gather(in_order(hidden, "dp"), "vocab").reshape(tokens, width)

    numbers = jnp.arange(block_owner.shape[0], dtype=jnp.int32)
    lane_index = jnp.arange(lane_count, dtype=jnp.int32)
    source = keep_ids[:, 0] // vocab_rows
    owner_before = (block_owner[None, :] == block_owner[:, None]) & (
        numbers[None, :] < numbers[:, None]
    )
    ordinal = jnp.sum(owner_before.astype(jnp.int32), axis=1)
    pair_rank = jnp.sum(
        (owner_before & (source[None, :] == source[:, None])).astype(jnp.int32), axis=1
    )
    send_slots = jnp.arange(shard_count * capacity, dtype=jnp.int32)
    outgoing = (
        (source == my_shard)[None, :]
        & (block_owner[None, :] == (send_slots // capacity)[:, None])
        & (pair_rank[None, :] == (send_slots % capacity)[:, None])
    )
    chosen = jnp.sum(jnp.where(outgoing, numbers[None, :], 0), axis=1)
    columns = jnp.clip(keep_ids[chosen] - my_shard * vocab_rows, 0, vocab_rows - 1)
    slot_counts = jnp.sum(jnp.where(outgoing, block_count[None, :], 0), axis=1)
    incoming = (block_owner[None, :] == my_shard) & (
        ordinal[None, :] == jnp.arange(kept_blocks, dtype=jnp.int32)[:, None]
    )
    own_blocks = jnp.sum(jnp.where(incoming, numbers[None, :], 0), axis=1)
    anchor = source[own_blocks] * (capacity + 1) + pair_rank[own_blocks]
    own_counts = block_count[own_blocks]
    valid = lane_index[None, :] < own_counts[:, None]

    picked = pick(teacher_logits, columns, slot_counts, shard_count, capacity)
    arrived = lax.all_to_all(picked, "vocab", split_axis=0, concat_axis=0, tiled=True)
    arrived, hidden = lax.optimization_barrier((arrived, hidden))
    target, mass_part = kept_probabilities(arrived, anchor, own_counts, capacity)
    mass_part = mass_part.reshape(-1)

    target = target.reshape(planes, part_blocks, lane_count, tok_rows)
    kept = []
    for distance in range(planes):
        piece = lax.dynamic_index_in_dim(target, above("dp", distance), 0, keepdims=False)
        kept.append(shift(piece, "dp", distance) if distance else piece)
    valid_cols = lax.dynamic_slice_in_dim(valid, plane * part_blocks, part_blocks).reshape(1, -1)

    scores = sum(
        jnp.dot(
            lax.dynamic_slice_in_dim(hidden, above("dp", -distance) * slab, slab, axis=1),
            piece, preferred_element_type=jnp.float32,
        )
        for distance, piece in enumerate(pieces)
    )
    masked = jnp.where(valid_cols, scores, -jnp.inf)
    local_top = jnp.max(masked, axis=1)
    weight = jnp.where(valid_cols, jnp.exp(masked - local_top[:, None]), 0.0)
    mass = jnp.where(
        jnp.arange(planes, dtype=jnp.int32)[None, :, None] == plane,
        mass_part.reshape(shard_count, 1, slice_rows), 0.0,
    ).reshape(tokens)
    student = jnp.stack([local_top, jnp.sum(weight, axis=1), mass])
    pieces, kept, student = lax.optimization_barrier((pieces, kept, student))
    origins = jnp.stack([above("dp", -distance) for distance in range(planes)])
    head, kept = place(origins, pieces, kept, shard_count)
    kept = kept.reshape(tokens, part_cols)
    student = exchange(student, ("dp", "vocab")).reshape(planes * shard_count, 3, tokens)
    student_top = jnp.max(student[:, 0], axis=0)
    exp_norm = jnp.sum(student[:, 1] * jnp.exp(student[:, 0] - student_top), axis=0)
    kept_mass = jnp.sum(student[:, 2], axis=0)
    factor = jnp.exp(local_top - student_top) / exp_norm * kept_mass
    gradient = (loss_scale * (weight * factor[:, None] - kept)).astype(jnp.bfloat16)

    gradients = [(plane, gradient)] + spread(gradient, "dp")

    by_pair = gradient.reshape(shard_count // 2, 2, planes * slice_rows, part_cols)

    def part(last_bit):
        rows = lax.dynamic_index_in_dim(by_pair, last_bit, 1, keepdims=False)
        product = lax.dot_general(
            rows.reshape(-1, part_cols), head, (((1,), (1,)), ((), ())),
            preferred_element_type=jnp.float32,
        )
        return product.reshape(shard_count // 2, planes, slice_rows, width)

    sums = direct_sum(part, "vocab")
    sums = lax.all_to_all(sums, "dp", split_axis=0, concat_axis=0, tiled=True)
    hidden_grad = jnp.sum(sums, axis=0).astype(jnp.bfloat16)

    own_hidden = lax.dynamic_slice_in_dim(hidden, plane * slab, slab, axis=1)
    head_grad = jnp.zeros((slab, own_cols), jnp.bfloat16)
    for origin, columns_part in gradients:
        block = lax.dot_general(
            own_hidden, columns_part, (((0,), (0,)), ((), ())),
            preferred_element_type=jnp.float32,
        ).astype(jnp.bfloat16)
        head_grad = lax.dynamic_update_slice_in_dim(head_grad, block, origin * part_cols, axis=1)
    return (head_grad, hidden_grad)


def solution(mesh):
    return jax.shard_map(
        shards,
        mesh=mesh,
        in_specs=(P("dp", "vocab"), P("dp", None), P("dp", "vocab"), P(), P(), P()),
        out_specs=(P("dp", "vocab"), P(("dp", "vocab"), None)),
        check_vma=False,
    )
```

```python
import functools

import jax
import jax.numpy as jnp
from jax import lax
from jax.experimental import pallas as pl
from jax.experimental.pallas import tpu as pltpu
from jax.sharding import PartitionSpec as P


loss_scale = 8192.0


def exchange(value, axes):
    count = lax.axis_size(axes)
    copies = jnp.broadcast_to(value[None], (count,) + value.shape)
    return lax.all_to_all(copies, axes, split_axis=0, concat_axis=0, tiled=True)


def shift(value, axis, distance):
    size = lax.axis_size(axis)
    return lax.ppermute(value, axis, [(p, (p + distance) % size) for p in range(size)])


def above(axis, distance):
    size = lax.axis_size(axis)
    return lax.rem(lax.axis_index(axis) + size + distance, size)


def chip_gather(value, axis):
    size = lax.axis_size(axis)
    index = lax.axis_index(axis)
    like = [value]
    for step in range(1, size // 2):
        like.append(lax.ppermute(value, axis, [(i, i ^ (2 * step)) for i in range(size)]))
    like = jnp.stack(like)
    other = lax.ppermute(like, axis, [(i, i ^ 1) for i in range(size)])
    both = jnp.stack([like, other], axis=1).reshape((size,) + value.shape)
    order = jnp.bitwise_xor(jnp.arange(size, dtype=jnp.int32), index)
    planes = value.shape[0]
    order = order[None, :] * planes + jnp.arange(planes, dtype=jnp.int32)[:, None]
    both = both.reshape((size * planes,) + value.shape[1:])
    return jnp.take(both, order.reshape(-1), axis=0, mode="clip")


def spread(value, axis):
    size = lax.axis_size(axis)
    index = lax.axis_index(axis)
    if size != 4:
        return [(above(axis, -d), shift(value, axis, d)) for d in range(1, size)]
    middle = shift(value, axis, 2)
    rising = lax.ppermute(value, axis, [(p, p + 1) for p in range(size - 1)])
    falling = lax.ppermute(value, axis, [(p + 1, p) for p in range(size - 1)])
    relay = lax.ppermute(middle, axis, [(1, 0), (2, 3)])
    first, last = index == 0, index == size - 1
    near = jnp.where(first, falling, rising)
    far = jnp.where(first | last, relay, falling)
    return [
        (jnp.where(first, 1, index - 1), near),
        (lax.rem(index + 2, size), middle),
        (jnp.where(first, size - 1, jnp.where(last, 0, index + 1)), far),
    ]


def direct_sum(gradient, head, axis):
    size = lax.axis_size(axis)
    index = lax.axis_index(axis)
    planes, _, rows, part_cols = gradient.shape
    pairs = gradient.reshape(planes, size // 2, 2, rows, part_cols).transpose(2, 1, 0, 3, 4)

    def product(part):
        out = lax.dot_general(
            part.reshape(-1, part_cols), head, (((1,), (1,)), ((), ())),
            preferred_element_type=jnp.float32,
        )
        return out.reshape(part.shape[:-1] + (head.shape[0],))

    away = product(lax.dynamic_index_in_dim(pairs, 1 - index % 2, 0, keepdims=False))
    near = lax.ppermute(away, axis, [(i, i ^ 1) for i in range(size)])
    own = lax.dynamic_index_in_dim(pairs, index % 2, 0, keepdims=False)

    def chip(place):
        part = product(lax.dynamic_index_in_dim(own, place, 0, keepdims=False))
        return part + lax.dynamic_index_in_dim(near, place, 0, keepdims=False)

    sends = [chip((index // 2) ^ step) for step in range(1, size // 2)]
    total = chip(index // 2)
    for step, send in enumerate(sends, 1):
        total = total + lax.ppermute(send, axis, [(i, i ^ (2 * step)) for i in range(size)])
    return total


def in_order(pieces, axis):
    size = len(pieces)
    order = lax.rem(lax.axis_index(axis) + size - jnp.arange(size, dtype=jnp.int32), size)
    return jnp.take(jnp.stack(pieces), order, axis=0, mode="clip")


def pick_kernel(capacity, ids_ref, count_ref, logits_ref, out_ref, wide_ref, rows_ref):
    vocab_rows, tok_rows = logits_ref.shape
    lanes = out_ref.shape[2]
    step = next(s for s in (400, 320, 160, 80, 16) if vocab_rows % s == 0)

    def widen(i, peak):
        rows = pl.ds(pl.multiple_of(i * step, step), step)
        part = logits_ref[rows, :].astype(jnp.float32)
        wide_ref[rows, :] = part
        return jnp.maximum(peak, jnp.max(part, axis=0, keepdims=True))

    peak = lax.fori_loop(0, vocab_rows // step, widen, jnp.full((1, tok_rows), -jnp.inf, jnp.float32))

    def add(i, total):
        rows = pl.ds(pl.multiple_of(i * step, step), step)
        return total + jnp.sum(jnp.exp(wide_ref[rows, :] - peak), axis=0, keepdims=True)

    total = lax.fori_loop(0, vocab_rows // step, add, jnp.zeros((1, tok_rows), jnp.float32))
    rows_ref[...] = jnp.zeros_like(rows_ref)
    first = total.astype(jnp.bfloat16).astype(jnp.float32)
    second = (total - first).astype(jnp.bfloat16).astype(jnp.float32)
    rows_ref[0:1, :] = peak
    rows_ref[1:2, :] = first
    rows_ref[2:3, :] = second
    rows_ref[3:4, :] = total - first - second
    terms = rows_ref[...].astype(out_ref.dtype)
    for shard in range(out_ref.shape[0]):
        out_ref[shard, capacity] = terms

    def slot(s, _):
        def eight(g, _):
            for j in range(8):
                row = ids_ref[s * lanes + g * 8 + j]
                rows_ref[pl.ds(g * 8 + j, 1), :] = wide_ref[pl.ds(row, 1), :]
            return 0

        @pl.when(count_ref[s] > 0)
        def _():
            lax.fori_loop(0, (count_ref[s] + 7) // 8, eight, 0)
            out_ref[s // capacity, s % capacity] = rows_ref[...].astype(out_ref.dtype)

        return 0

    lax.fori_loop(0, out_ref.shape[0] * capacity, slot, 0)


def pick(teacher_logits, ids, counts, shards, capacity):
    tok_rows, vocab_rows = teacher_logits.shape
    lanes = ids.shape[1]
    return pl.pallas_call(
        functools.partial(pick_kernel, capacity),
        out_shape=jax.ShapeDtypeStruct(
            (shards, capacity + 1, lanes, tok_rows), teacher_logits.dtype
        ),
        in_specs=[
            pl.BlockSpec(memory_space=pltpu.SMEM),
            pl.BlockSpec(memory_space=pltpu.SMEM),
            pl.BlockSpec(memory_space=pltpu.VMEM),
        ],
        out_specs=pl.BlockSpec(memory_space=pltpu.VMEM),
        scratch_shapes=[
            pltpu.VMEM((vocab_rows, tok_rows), jnp.float32),
            pltpu.VMEM((lanes, tok_rows), jnp.float32),
        ],
    )(ids.reshape(-1), counts, teacher_logits.T)


def kept_kernel(capacity, anchor_ref, count_ref, arrived_ref, kept_ref, mass_ref):
    shards = arrived_ref.shape[0] // (capacity + 1)
    tops, sums = [], []
    for shard in range(shards):
        terms = arrived_ref[shard * (capacity + 1) + capacity, 0:16, :].astype(jnp.float32)
        tops.append(terms[0:1])
        sums.append(terms[1:2] + terms[2:3] + terms[3:4])
    peak = functools.reduce(jnp.maximum, tops)
    total = sum(part * jnp.exp(top - peak) for top, part in zip(tops, sums))
    lane = lax.broadcasted_iota(jnp.int32, kept_ref.shape[1:], 0)

    def block(b, mass):
        logits = arrived_ref[anchor_ref[b]].astype(jnp.float32)
        probs = jnp.where(lane < count_ref[b], jnp.exp(logits - peak) / total, 0.0)
        kept = probs.astype(kept_ref.dtype)
        kept_ref[b] = kept
        return mass + jnp.sum(kept.astype(jnp.float32), axis=0, keepdims=True)

    mass_ref[...] = lax.fori_loop(0, kept_ref.shape[0], block, jnp.zeros(mass_ref.shape, jnp.float32))


def kept_probabilities(arrived, anchor, counts, capacity):
    lanes, tok_rows = arrived.shape[2:]
    return pl.pallas_call(
        functools.partial(kept_kernel, capacity),
        out_shape=(
            jax.ShapeDtypeStruct((anchor.shape[0], lanes, tok_rows), arrived.dtype),
            jax.ShapeDtypeStruct((1, tok_rows), jnp.float32),
        ),
        in_specs=[
            pl.BlockSpec(memory_space=pltpu.SMEM),
            pl.BlockSpec(memory_space=pltpu.SMEM),
            pl.BlockSpec(memory_space=pltpu.VMEM),
        ],
        out_specs=[pl.BlockSpec(memory_space=pltpu.VMEM)] * 2,
    )(anchor, counts, arrived.reshape(-1, lanes, tok_rows))


def place_kernel(planes, origin_ref, *refs):
    heads, kepts, (head_ref, kept_ref) = refs[:planes], refs[planes : 2 * planes], refs[2 * planes :]
    for distance in range(planes):
        origin = origin_ref[distance]
        slab, _ = heads[distance].shape
        head_ref[pl.ds(pl.multiple_of(origin * slab, 16), slab), :] = heads[distance][...]
        blocks, lanes, _ = kepts[distance].shape
        for block in range(blocks):
            tile = kepts[distance][block].astype(jnp.float32).T
            columns = slice(block * lanes, (block + 1) * lanes)
            kept_ref[pl.ds(origin, 1), :, columns] = tile[None]


def place(origins, heads, kepts):
    planes = len(heads)
    slab, part_cols = heads[0].shape
    vmem = pl.BlockSpec(memory_space=pltpu.VMEM)
    return pl.pallas_call(
        functools.partial(place_kernel, planes),
        out_shape=(
            jax.ShapeDtypeStruct((planes * slab, part_cols), heads[0].dtype),
            jax.ShapeDtypeStruct((planes, kepts[0].shape[2], part_cols), jnp.float32),
        ),
        in_specs=[pl.BlockSpec(memory_space=pltpu.SMEM)] + [vmem] * (2 * planes),
        out_specs=[vmem] * 2,
    )(origins, *heads, *kepts)


def shards(teacher_logits, student_hidden, student_head, keep_ids, block_owner, block_count):
    planes = lax.axis_size("dp")
    plane = lax.axis_index("dp")
    shard_count = lax.axis_size("vocab")
    my_shard = lax.axis_index("vocab")
    tok_rows, vocab_rows = teacher_logits.shape
    slab, own_cols = student_head.shape
    width = student_hidden.shape[1]
    lane_count = keep_ids.shape[1]
    kept_blocks = block_owner.shape[0] // shard_count
    part_blocks = kept_blocks // planes
    part_cols = own_cols // planes
    slice_rows = tok_rows // shard_count
    tokens = planes * tok_rows
    capacity = (2 * kept_blocks + shard_count - 1) // shard_count

    pieces = []
    for distance in range(planes):
        piece = lax.dynamic_slice_in_dim(
            student_head, above("dp", distance) * part_cols, part_cols, 1
        )
        pieces.append(shift(piece, "dp", distance) if distance else piece)

    hidden_slice = lax.dynamic_slice_in_dim(student_hidden, my_shard * slice_rows, slice_rows)
    hidden = [shift(hidden_slice, "dp", d) if d else hidden_slice for d in range(planes)]
    hidden = chip_gather(in_order(hidden, "dp"), "vocab").reshape(tokens, width)

    numbers = jnp.arange(block_owner.shape[0], dtype=jnp.int32)
    lane_index = jnp.arange(lane_count, dtype=jnp.int32)
    source = keep_ids[:, 0] // vocab_rows
    owner_before = (block_owner[None, :] == block_owner[:, None]) & (
        numbers[None, :] < numbers[:, None]
    )
    ordinal = jnp.sum(owner_before.astype(jnp.int32), axis=1)
    pair_rank = jnp.sum(
        (owner_before & (source[None, :] == source[:, None])).astype(jnp.int32), axis=1
    )
    send_slots = jnp.arange(shard_count * capacity, dtype=jnp.int32)
    outgoing = (
        (source == my_shard)[None, :]
        & (block_owner[None, :] == (send_slots // capacity)[:, None])
        & (pair_rank[None, :] == (send_slots % capacity)[:, None])
    )
    chosen = jnp.sum(jnp.where(outgoing, numbers[None, :], 0), axis=1)
    columns = jnp.clip(keep_ids[chosen] - my_shard * vocab_rows, 0, vocab_rows - 1)
    slot_counts = jnp.sum(jnp.where(outgoing, block_count[None, :], 0), axis=1)
    incoming = (block_owner[None, :] == my_shard) & (
        ordinal[None, :] == jnp.arange(kept_blocks, dtype=jnp.int32)[:, None]
    )
    own_blocks = jnp.sum(jnp.where(incoming, numbers[None, :], 0), axis=1)
    anchor = source[own_blocks] * (capacity + 1) + pair_rank[own_blocks]
    own_counts = block_count[own_blocks]
    valid = lane_index[None, :] < own_counts[:, None]

    picked = pick(teacher_logits, columns, slot_counts, shard_count, capacity)
    arrived = lax.all_to_all(picked, "vocab", split_axis=0, concat_axis=0, tiled=True)
    arrived, hidden = lax.optimization_barrier((arrived, hidden))
    target, mass_part = kept_probabilities(arrived, anchor, own_counts, capacity)
    mass_part = mass_part.reshape(-1)

    target = target.reshape(planes, part_blocks, lane_count, tok_rows)
    kept = []
    for distance in range(planes):
        piece = lax.dynamic_index_in_dim(target, above("dp", distance), 0, keepdims=False)
        kept.append(shift(piece, "dp", distance) if distance else piece)
    valid_cols = lax.dynamic_slice_in_dim(valid, plane * part_blocks, part_blocks).reshape(1, -1)

    scores = sum(
        jnp.dot(
            lax.dynamic_slice_in_dim(hidden, above("dp", -distance) * slab, slab, axis=1),
            piece, preferred_element_type=jnp.float32,
        )
        for distance, piece in enumerate(pieces)
    )
    masked = jnp.where(valid_cols, scores, -jnp.inf)
    local_top = jnp.max(masked, axis=1)
    weight = jnp.where(valid_cols, jnp.exp(masked - local_top[:, None]), 0.0)
    mass = lax.dynamic_update_slice_in_dim(
        jnp.zeros((tokens,), jnp.float32), mass_part, plane * tok_rows, 0
    )
    student = jnp.stack([local_top, jnp.sum(weight, axis=1), mass])
    pieces, kept, student = lax.optimization_barrier((pieces, kept, student))
    origins = jnp.stack([above("dp", -distance) for distance in range(planes)])
    head, kept = place(origins, pieces, kept)
    kept = kept.reshape(tokens, part_cols)
    student = exchange(student, ("dp", "vocab")).reshape(planes * shard_count, 3, tokens)
    student_top = jnp.max(student[:, 0], axis=0)
    exp_norm = jnp.sum(student[:, 1] * jnp.exp(student[:, 0] - student_top), axis=0)
    kept_mass = jnp.sum(student[:, 2], axis=0)
    factor = jnp.exp(local_top - student_top) / exp_norm * kept_mass
    gradient = (loss_scale * (weight * factor[:, None] - kept)).astype(jnp.bfloat16)

    gradients = [(plane, gradient)] + spread(gradient, "dp")

    sums = direct_sum(
        gradient.reshape(planes, shard_count, slice_rows, part_cols), head, "vocab"
    )
    sums = lax.all_to_all(sums, "dp", split_axis=0, concat_axis=0, tiled=True)
    hidden_grad = jnp.sum(sums, axis=0).astype(jnp.bfloat16)

    own_hidden = lax.dynamic_slice_in_dim(hidden, plane * slab, slab, axis=1)
    head_grad = jnp.zeros((slab, own_cols), jnp.bfloat16)
    for origin, columns_part in gradients:
        block = lax.dot_general(
            own_hidden, columns_part, (((0,), (0,)), ((), ())),
            preferred_element_type=jnp.float32,
        ).astype(jnp.bfloat16)
        head_grad = lax.dynamic_update_slice_in_dim(head_grad, block, origin * part_cols, axis=1)
    return (head_grad, hidden_grad)


def solution(mesh):
    return jax.shard_map(
        shards,
        mesh=mesh,
        in_specs=(P("dp", "vocab"), P("dp", None), P("dp", "vocab"), P(), P(), P()),
        out_specs=(P("dp", "vocab"), P(("dp", "vocab"), None)),
        check_vma=False,
    )
```

```python
import functools

import jax
import jax.numpy as jnp
from jax import lax
from jax.experimental import pallas as pl
from jax.experimental.pallas import tpu as pltpu
from jax.sharding import PartitionSpec as P


loss_scale = 8192.0


def exchange(value, axes):
    count = lax.axis_size(axes)
    copies = jnp.broadcast_to(value[None], (count,) + value.shape)
    return lax.all_to_all(copies, axes, split_axis=0, concat_axis=0, tiled=True)


def shift(value, axis, distance):
    size = lax.axis_size(axis)
    return lax.ppermute(value, axis, [(p, (p + distance) % size) for p in range(size)])


def above(axis, distance):
    size = lax.axis_size(axis)
    return lax.rem(lax.axis_index(axis) + size + distance, size)


def chip_gather(value, axis):
    size = lax.axis_size(axis)
    index = lax.axis_index(axis)
    like = [value]
    for step in range(1, size // 2):
        like.append(lax.ppermute(value, axis, [(i, i ^ (2 * step)) for i in range(size)]))
    like = jnp.stack(like)
    other = lax.ppermute(like, axis, [(i, i ^ 1) for i in range(size)])
    both = jnp.stack([like, other], axis=1).reshape((size,) + value.shape)
    order = jnp.bitwise_xor(jnp.arange(size, dtype=jnp.int32), index)
    planes = value.shape[0]
    order = order[None, :] * planes + jnp.arange(planes, dtype=jnp.int32)[:, None]
    both = both.reshape((size * planes,) + value.shape[1:])
    return jnp.take(both, order.reshape(-1), axis=0, mode="clip")


def spread(value, axis):
    size = lax.axis_size(axis)
    index = lax.axis_index(axis)
    if size != 4:
        return [(above(axis, -d), shift(value, axis, d)) for d in range(1, size)]
    middle = shift(value, axis, 2)
    rising = lax.ppermute(value, axis, [(p, p + 1) for p in range(size - 1)])
    falling = lax.ppermute(value, axis, [(p + 1, p) for p in range(size - 1)])
    relay = lax.ppermute(middle, axis, [(1, 0), (2, 3)])
    first, last = index == 0, index == size - 1
    near = jnp.where(first, falling, rising)
    far = jnp.where(first | last, relay, falling)
    return [
        (jnp.where(first, 1, index - 1), near),
        (lax.rem(index + 2, size), middle),
        (jnp.where(first, size - 1, jnp.where(last, 0, index + 1)), far),
    ]


def direct_sum(gradient, head, axis):
    size = lax.axis_size(axis)
    index = lax.axis_index(axis)
    planes, _, rows, part_cols = gradient.shape
    pairs = gradient.reshape(planes, size // 2, 2, rows, part_cols).transpose(2, 1, 0, 3, 4)

    def product(part):
        out = lax.dot_general(
            part.reshape(-1, part_cols), head, (((1,), (1,)), ((), ())),
            preferred_element_type=jnp.float32,
        )
        return out.reshape(part.shape[:-1] + (head.shape[0],))

    away = product(lax.dynamic_index_in_dim(pairs, 1 - index % 2, 0, keepdims=False))
    near = lax.ppermute(away, axis, [(i, i ^ 1) for i in range(size)])
    own = lax.dynamic_index_in_dim(pairs, index % 2, 0, keepdims=False)

    def chip(place):
        part = product(lax.dynamic_index_in_dim(own, place, 0, keepdims=False))
        return part + lax.dynamic_index_in_dim(near, place, 0, keepdims=False)

    sends = [chip((index // 2) ^ step) for step in range(1, size // 2)]
    total = chip(index // 2)
    for step, send in enumerate(sends, 1):
        total = total + lax.ppermute(send, axis, [(i, i ^ (2 * step)) for i in range(size)])
    return total


def in_order(pieces, axis):
    size = len(pieces)
    order = lax.rem(lax.axis_index(axis) + size - jnp.arange(size, dtype=jnp.int32), size)
    return jnp.take(jnp.stack(pieces), order, axis=0, mode="clip")


def pick_kernel(capacity, ids_ref, count_ref, logits_ref, out_ref, wide_ref, rows_ref):
    vocab_rows, tok_rows = logits_ref.shape
    lanes = out_ref.shape[2]
    step = next(s for s in (400, 320, 160, 80, 16) if vocab_rows % s == 0)

    def widen(i, peak):
        rows = pl.ds(pl.multiple_of(i * step, step), step)
        part = logits_ref[rows, :].astype(jnp.float32)
        wide_ref[rows, :] = part
        return jnp.maximum(peak, jnp.max(part, axis=0, keepdims=True))

    peak = lax.fori_loop(0, vocab_rows // step, widen, jnp.full((1, tok_rows), -jnp.inf, jnp.float32))

    def add(i, total):
        rows = pl.ds(pl.multiple_of(i * step, step), step)
        return total + jnp.sum(jnp.exp(wide_ref[rows, :] - peak), axis=0, keepdims=True)

    total = lax.fori_loop(0, vocab_rows // step, add, jnp.zeros((1, tok_rows), jnp.float32))
    rows_ref[...] = jnp.zeros_like(rows_ref)
    first = total.astype(jnp.bfloat16).astype(jnp.float32)
    second = (total - first).astype(jnp.bfloat16).astype(jnp.float32)
    rows_ref[0:1, :] = peak
    rows_ref[1:2, :] = first
    rows_ref[2:3, :] = second
    rows_ref[3:4, :] = total - first - second
    terms = rows_ref[...].astype(out_ref.dtype)
    for shard in range(out_ref.shape[0]):
        out_ref[shard, capacity] = terms

    def slot(s, _):
        def eight(g, _):
            for j in range(8):
                row = ids_ref[s * lanes + g * 8 + j]
                rows_ref[pl.ds(g * 8 + j, 1), :] = wide_ref[pl.ds(row, 1), :]
            return 0

        @pl.when(count_ref[s] > 0)
        def _():
            lax.fori_loop(0, (count_ref[s] + 7) // 8, eight, 0)
            out_ref[s // capacity, s % capacity] = rows_ref[...].astype(out_ref.dtype)

        return 0

    lax.fori_loop(0, out_ref.shape[0] * capacity, slot, 0)


def pick(teacher_logits, ids, counts, shards, capacity):
    tok_rows, vocab_rows = teacher_logits.shape
    lanes = ids.shape[1]
    return pl.pallas_call(
        functools.partial(pick_kernel, capacity),
        out_shape=jax.ShapeDtypeStruct(
            (shards, capacity + 1, lanes, tok_rows), teacher_logits.dtype
        ),
        in_specs=[
            pl.BlockSpec(memory_space=pltpu.SMEM),
            pl.BlockSpec(memory_space=pltpu.SMEM),
            pl.BlockSpec(memory_space=pltpu.VMEM),
        ],
        out_specs=pl.BlockSpec(memory_space=pltpu.VMEM),
        scratch_shapes=[
            pltpu.VMEM((vocab_rows, tok_rows), jnp.float32),
            pltpu.VMEM((lanes, tok_rows), jnp.float32),
        ],
    )(ids.reshape(-1), counts, teacher_logits.T)


def kept_kernel(capacity, anchor_ref, count_ref, arrived_ref, kept_ref, mass_ref):
    shards = arrived_ref.shape[0] // (capacity + 1)
    tops, sums = [], []
    for shard in range(shards):
        terms = arrived_ref[shard * (capacity + 1) + capacity, 0:16, :].astype(jnp.float32)
        tops.append(terms[0:1])
        sums.append(terms[1:2] + terms[2:3] + terms[3:4])
    peak = functools.reduce(jnp.maximum, tops)
    total = sum(part * jnp.exp(top - peak) for top, part in zip(tops, sums))
    lane = lax.broadcasted_iota(jnp.int32, kept_ref.shape[1:], 0)

    def block(b, mass):
        logits = arrived_ref[anchor_ref[b]].astype(jnp.float32)
        probs = jnp.where(lane < count_ref[b], jnp.exp(logits - peak) / total, 0.0)
        kept = probs.astype(kept_ref.dtype)
        kept_ref[b] = kept
        return mass + jnp.sum(kept.astype(jnp.float32), axis=0, keepdims=True)

    mass_ref[...] = lax.fori_loop(0, kept_ref.shape[0], block, jnp.zeros(mass_ref.shape, jnp.float32))


def kept_probabilities(arrived, anchor, counts, capacity):
    lanes, tok_rows = arrived.shape[2:]
    return pl.pallas_call(
        functools.partial(kept_kernel, capacity),
        out_shape=(
            jax.ShapeDtypeStruct((anchor.shape[0], lanes, tok_rows), arrived.dtype),
            jax.ShapeDtypeStruct((1, tok_rows), jnp.float32),
        ),
        in_specs=[
            pl.BlockSpec(memory_space=pltpu.SMEM),
            pl.BlockSpec(memory_space=pltpu.SMEM),
            pl.BlockSpec(memory_space=pltpu.VMEM),
        ],
        out_specs=[pl.BlockSpec(memory_space=pltpu.VMEM)] * 2,
    )(anchor, counts, arrived.reshape(-1, lanes, tok_rows))


def place_kernel(planes, origin_ref, *refs):
    heads, kepts, (head_ref, kept_ref) = refs[:planes], refs[planes : 2 * planes], refs[2 * planes :]
    for distance in range(planes):
        origin = origin_ref[distance]
        slab, _ = heads[distance].shape
        head_ref[pl.ds(pl.multiple_of(origin * slab, 16), slab), :] = heads[distance][...]
        blocks, lanes, _ = kepts[distance].shape
        for block in range(blocks):
            tile = kepts[distance][block].astype(jnp.float32).T
            columns = slice(block * lanes, (block + 1) * lanes)
            kept_ref[pl.ds(origin, 1), :, columns] = tile[None]


def place(origins, heads, kepts):
    planes = len(heads)
    slab, part_cols = heads[0].shape
    vmem = pl.BlockSpec(memory_space=pltpu.VMEM)
    return pl.pallas_call(
        functools.partial(place_kernel, planes),
        out_shape=(
            jax.ShapeDtypeStruct((planes * slab, part_cols), heads[0].dtype),
            jax.ShapeDtypeStruct((planes, kepts[0].shape[2], part_cols), jnp.float32),
        ),
        in_specs=[pl.BlockSpec(memory_space=pltpu.SMEM)] + [vmem] * (2 * planes),
        out_specs=[vmem] * 2,
    )(origins, *heads, *kepts)


def shards(teacher_logits, student_hidden, student_head, keep_ids, block_owner, block_count):
    planes = lax.axis_size("dp")
    plane = lax.axis_index("dp")
    shard_count = lax.axis_size("vocab")
    my_shard = lax.axis_index("vocab")
    tok_rows, vocab_rows = teacher_logits.shape
    slab, own_cols = student_head.shape
    width = student_hidden.shape[1]
    lane_count = keep_ids.shape[1]
    kept_blocks = block_owner.shape[0] // shard_count
    part_blocks = kept_blocks // planes
    part_cols = own_cols // planes
    slice_rows = tok_rows // shard_count
    tokens = planes * tok_rows
    capacity = (2 * kept_blocks + shard_count - 1) // shard_count

    def columns_of(head, distance):
        return lax.dynamic_slice_in_dim(head, above("dp", distance) * part_cols, part_cols, 1)

    first = columns_of(student_head, 1)
    first, later = lax.optimization_barrier((first, student_head))
    pieces = [columns_of(later, 0)]
    for distance in range(1, planes):
        piece = columns_of(later, distance) if distance > 1 else first
        pieces.append(shift(piece, "dp", distance))

    hidden_slice = lax.dynamic_slice_in_dim(student_hidden, my_shard * slice_rows, slice_rows)
    hidden = [shift(hidden_slice, "dp", d) if d else hidden_slice for d in range(planes)]
    hidden = chip_gather(in_order(hidden, "dp"), "vocab").reshape(tokens, width)

    numbers = jnp.arange(block_owner.shape[0], dtype=jnp.int32)
    lane_index = jnp.arange(lane_count, dtype=jnp.int32)
    source = keep_ids[:, 0] // vocab_rows
    owner_before = (block_owner[None, :] == block_owner[:, None]) & (
        numbers[None, :] < numbers[:, None]
    )
    ordinal = jnp.sum(owner_before.astype(jnp.int32), axis=1)
    pair_rank = jnp.sum(
        (owner_before & (source[None, :] == source[:, None])).astype(jnp.int32), axis=1
    )
    send_slots = jnp.arange(shard_count * capacity, dtype=jnp.int32)
    outgoing = (
        (source == my_shard)[None, :]
        & (block_owner[None, :] == (send_slots // capacity)[:, None])
        & (pair_rank[None, :] == (send_slots % capacity)[:, None])
    )
    chosen = jnp.sum(jnp.where(outgoing, numbers[None, :], 0), axis=1)
    columns = jnp.clip(keep_ids[chosen] - my_shard * vocab_rows, 0, vocab_rows - 1)
    slot_counts = jnp.sum(jnp.where(outgoing, block_count[None, :], 0), axis=1)
    incoming = (block_owner[None, :] == my_shard) & (
        ordinal[None, :] == jnp.arange(kept_blocks, dtype=jnp.int32)[:, None]
    )
    own_blocks = jnp.sum(jnp.where(incoming, numbers[None, :], 0), axis=1)
    anchor = source[own_blocks] * (capacity + 1) + pair_rank[own_blocks]
    own_counts = block_count[own_blocks]
    valid = lane_index[None, :] < own_counts[:, None]

    picked = pick(teacher_logits, columns, slot_counts, shard_count, capacity)
    arrived = lax.all_to_all(picked, "vocab", split_axis=0, concat_axis=0, tiled=True)
    arrived, hidden = lax.optimization_barrier((arrived, hidden))
    target, mass_part = kept_probabilities(arrived, anchor, own_counts, capacity)
    mass_part = mass_part.reshape(-1)

    target = target.reshape(planes, part_blocks, lane_count, tok_rows)
    kept = []
    for distance in range(planes):
        piece = lax.dynamic_index_in_dim(target, above("dp", distance), 0, keepdims=False)
        kept.append(shift(piece, "dp", distance) if distance else piece)
    valid_cols = lax.dynamic_slice_in_dim(valid, plane * part_blocks, part_blocks).reshape(1, -1)

    scores = 0.0
    for distance, piece in enumerate(pieces):
        rows = lax.dynamic_slice_in_dim(hidden, above("dp", -distance) * slab, slab, axis=1)
        scores = scores + jnp.dot(rows, piece, preferred_element_type=jnp.float32)
    masked = jnp.where(valid_cols, scores, -jnp.inf)
    local_top = jnp.max(masked, axis=1)
    weight = jnp.where(valid_cols, jnp.exp(masked - local_top[:, None]), 0.0)
    mass = lax.dynamic_update_slice_in_dim(
        jnp.zeros((tokens,), jnp.float32), mass_part, plane * tok_rows, 0
    )
    student = jnp.stack([local_top, jnp.sum(weight, axis=1), mass])
    pieces, kept, _ = lax.optimization_barrier((pieces, kept, student))
    origins = jnp.stack([above("dp", -distance) for distance in range(planes)])
    head, kept = place(origins, pieces, kept)
    kept = kept.reshape(tokens, part_cols)
    student = exchange(student, ("dp", "vocab")).reshape(planes * shard_count, 3, tokens)
    student_top = jnp.max(student[:, 0], axis=0)
    exp_norm = jnp.sum(student[:, 1] * jnp.exp(student[:, 0] - student_top), axis=0)
    kept_mass = jnp.sum(student[:, 2], axis=0)
    factor = jnp.exp(local_top - student_top) / exp_norm * kept_mass
    gradient = (loss_scale * (weight * factor[:, None] - kept)).astype(jnp.bfloat16)

    gradients = [(plane, gradient)] + spread(gradient, "dp")

    sums = direct_sum(
        gradient.reshape(planes, shard_count, slice_rows, part_cols), head, "vocab"
    )
    sums = lax.all_to_all(sums, "dp", split_axis=0, concat_axis=0, tiled=True)
    hidden_grad = jnp.sum(sums, axis=0).astype(jnp.bfloat16)

    own_hidden = lax.dynamic_slice_in_dim(hidden, plane * slab, slab, axis=1)
    head_grad = jnp.zeros((slab, own_cols), jnp.bfloat16)
    for origin, columns_part in gradients:
        block = lax.dot_general(
            own_hidden, columns_part, (((0,), (0,)), ((), ())),
            preferred_element_type=jnp.float32,
        ).astype(jnp.bfloat16)
        head_grad = lax.dynamic_update_slice_in_dim(head_grad, block, origin * part_cols, axis=1)
    return (head_grad, hidden_grad)


def solution(mesh):
    return jax.shard_map(
        shards,
        mesh=mesh,
        in_specs=(P("dp", "vocab"), P("dp", None), P("dp", "vocab"), P(), P(), P()),
        out_specs=(P("dp", "vocab"), P(("dp", "vocab"), None)),
        check_vma=False,
    )
```
